32 devices in a mesh: groups: 2 (over y), tensor: 4 (over z), dp: 4 (over x, core).
Axes of the slice: x: 2, y: 2, z: 4, core: 2. Of those that a mesh axis runs over, the one named last changes fastest.
Arguments:
- tokens: bfloat16 [256, 8192], P(('groups', 'tensor', 'dp')), parts along dimension 0, may hold values from -6 to 6
- gate_projection_matrix: bfloat16 [8192, 14336], P('dp', 'tensor'), may hold values from -0.0625 to 0.0625
- up_projection_matrix: bfloat16 [8192, 14336], P('dp', 'tensor'), may hold values from -0.0625 to 0.0625
- down_projection_matrix: bfloat16 [14336, 8192], P('tensor', 'dp'), may hold values from -0.046875 to 0.046875
- gate_adapter_inmap: bfloat16 [16384, 64], P(('groups', 'dp')), parts along dimension 0, may hold values from -0.0625 to 0.0625
- gate_adapter_outmap: bfloat16 [64, 28672], P(None, ('groups', 'tensor')), parts along dimension 1, may hold values from -0.75 to 0.75
- up_adapter_inmap: bfloat16 [16384, 64], P(('groups', 'dp')), parts along dimension 0, may hold values from -0.0625 to 0.0625
- up_adapter_outmap: bfloat16 [64, 28672], P(None, ('groups', 'tensor')), parts along dimension 1, may hold values from -0.75 to 0.75
- down_adapter_inmap: bfloat16 [28672, 64], P(('groups', 'tensor')), parts along dimension 0, may hold values from -0.046875 to 0.046875
- down_adapter_outmap: bfloat16 [64, 16384], P(None, 'groups'), parts along dimension 1, may hold values from -0.75 to 0.75
Outputs:
- block_out: bfloat16 [256, 8192], P(('groups', 'tensor', 'dp')), parts along dimension 0
The draws below stay inside these ranges and needn't reach their ends.
There are 2 independent parts, one for each index of `groups`. The reference program is written for one: setup_inputs(seed, part) draws one part's arguments, and reference() takes and returns one part's arrays. A program takes and returns all parts, laid end to end along the dimension named above; an argument that names none is the same for every part. Nothing has to cross between parts.
All inputs are finite; a program needn't handle non-finite values.
Results may differ from the reference program's by a relative error of at most 0.0053.
Values may be sent and summed in bfloat16 or wider, within the bound.
A program may use at most 256 MiB of HBM per device.

```python
import jax
import jax.numpy as jnp
from jax import lax

MODEL_WIDTH = 8192
HIDDEN_UNITS = 14336
ADAPTER_RANK = 64
TOKENS = 128


def steps_of(stream_key, shape, split, smallest, top_value):
    loudness = 1.0
    for position, blocks in split:
        draws = jax.random.uniform(jax.random.fold_in(jax.random.fold_in(stream_key, 6), position), (blocks,), jnp.float32, smallest / len(split), top_value / len(split))
        loudness = loudness * jnp.repeat(jnp.exp(draws), shape[position] // blocks).reshape((-1,) + (1,) * (len(shape) - 1 - position))
    return loudness


def noise(stream_key, shape, width, reach, shards=(), held_as=jnp.bfloat16):
    gain = steps_of(stream_key, shape, shards, -0.22, 0.18) if shards else 1.0
    result = jax.random.normal(stream_key, shape, jnp.float32) * width * gain
    return jnp.minimum(jnp.maximum(result, -reach), reach).astype(held_as)


def setup_inputs(seed: int = 0, part: int = 0) -> dict:
    keys = jax.random.split(jax.random.key(seed), 11)
    own_keys = jax.random.split(jax.random.fold_in(keys[10], part), 11)
    tokens = noise(own_keys[0], (TOKENS, MODEL_WIDTH), 1.0, 6.0, ((0, 16),))
    gate_projection_matrix = noise(keys[1], (MODEL_WIDTH, HIDDEN_UNITS), MODEL_WIDTH ** -0.5, 0.0625, ((0, 4), (1, 4)))
    up_projection_matrix = noise(keys[2], (MODEL_WIDTH, HIDDEN_UNITS), MODEL_WIDTH ** -0.5, 0.0625, ((0, 4), (1, 4)))
    down_projection_matrix = noise(keys[3], (HIDDEN_UNITS, MODEL_WIDTH), HIDDEN_UNITS ** -0.5, 0.046875, ((0, 4), (1, 4)))
    gate_adapter_inmap = noise(own_keys[4], (MODEL_WIDTH, ADAPTER_RANK), MODEL_WIDTH ** -0.5, 0.0625, ((0, 4),))
    gate_adapter_outmap = noise(own_keys[5], (ADAPTER_RANK, HIDDEN_UNITS), ADAPTER_RANK ** -0.5, 0.75, ((1, 4),))
    up_adapter_inmap = noise(own_keys[6], (MODEL_WIDTH, ADAPTER_RANK), MODEL_WIDTH ** -0.5, 0.0625, ((0, 4),))
    up_adapter_outmap = noise(own_keys[7], (ADAPTER_RANK, HIDDEN_UNITS), ADAPTER_RANK ** -0.5, 0.75, ((1, 4),))
    down_adapter_inmap = noise(own_keys[8], (HIDDEN_UNITS, ADAPTER_RANK), HIDDEN_UNITS ** -0.5, 0.046875, ((0, 4),))
    down_adapter_outmap = noise(own_keys[9], (ADAPTER_RANK, MODEL_WIDTH), ADAPTER_RANK ** -0.5, 0.75)
    return dict(tokens=tokens, gate_projection_matrix=gate_projection_matrix, up_projection_matrix=up_projection_matrix, down_projection_matrix=down_projection_matrix, gate_adapter_inmap=gate_adapter_inmap, gate_adapter_outmap=gate_adapter_outmap, up_adapter_inmap=up_adapter_inmap, up_adapter_outmap=up_adapter_outmap, down_adapter_inmap=down_adapter_inmap, down_adapter_outmap=down_adapter_outmap)


adapter_scale_factor = 0.5


def reference(tokens, gate_projection_matrix, up_projection_matrix, down_projection_matrix, gate_adapter_inmap, gate_adapter_outmap, up_adapter_inmap, up_adapter_outmap, down_adapter_inmap, down_adapter_outmap):
    gate_lowrank_part = jnp.dot(tokens, gate_adapter_inmap, preferred_element_type=jnp.float32).astype(jnp.bfloat16)
    up_lowrank_part = jnp.dot(tokens, up_adapter_inmap, preferred_element_type=jnp.float32).astype(jnp.bfloat16)
    gate_activated = jnp.dot(tokens, gate_projection_matrix, preferred_element_type=jnp.float32) + adapter_scale_factor * jnp.dot(gate_lowrank_part, gate_adapter_outmap, preferred_element_type=jnp.float32)
    up_projected_value = jnp.dot(tokens, up_projection_matrix, preferred_element_type=jnp.float32) + adapter_scale_factor * jnp.dot(up_lowrank_part, up_adapter_outmap, preferred_element_type=jnp.float32)
    hidden_product = (jax.nn.silu(gate_activated) * up_projected_value).astype(jnp.bfloat16)
    down_lowrank_part = jnp.dot(hidden_product, down_adapter_inmap, preferred_element_type=jnp.float32)
    block_result_rows = jnp.dot(hidden_product, down_projection_matrix, preferred_element_type=jnp.float32)
    block_result_rows = block_result_rows + adapter_scale_factor * jnp.dot(down_lowrank_part, down_adapter_outmap.astype(jnp.float32), precision=lax.Precision.HIGHEST)
    return block_result_rows.astype(jnp.bfloat16)
```

```python
import functools

import jax
import jax.numpy as jnp
from jax import lax
from jax.experimental import pallas as pl
from jax.experimental.pallas import tpu as pltpu
from jax.sharding import PartitionSpec as P

adapter_scale_factor = 0.5
MESH = pl.DeviceIdType.MESH
HALVES = 2
SUM_LAG, ACT_LAG, FWD_LAG, DOWN_LAG = 2, 6, 9, 11


def dot_rows(a, b):
    return lax.dot_general(a, b, (((1,), (1,)), ((), ())), preferred_element_type=jnp.float32)


def kernel(
    nt, nd, nc,
    tok, wg, wu, wd, ag, go, au, uo, di, do, out,
    tokv, xbuf, x, wgv, wuv, wdv, agv, auv, gov, uov, div, dov,
    lowp, lowr, lowb, part, send_a, recv_a, send_b, recv_b, hid, acc, dl,
    osend, orecv, fin, straight, land,
    wsem, ssem, tok_s, tok_r, low_s, low_r, a_s, a_r, b_s, b_r,
    h_s, h_r, p_s, p_r, f_s, f_r, o_s, o_r, z_s, z_r, l_s, l_r,
):
    n = nt * nd
    half = nd // 2
    depth = wg.shape[0]
    chunk = wgv.shape[2]
    width = wd.shape[1]
    rank = agv.shape[0]
    tok_dev = tok.shape[0]
    total_rows = n * tok_dev
    side = total_rows // HALVES
    rows = side // nd
    owners = nd // HALVES
    block = owners * tok_dev
    slots = nt * owners
    per_block = slots // nd
    items = HALVES * nc
    my_t = lax.axis_index("tensor")
    my_d = lax.axis_index("dp")
    me = my_t * nd + my_d
    my_j = lax.div(my_d, 2)
    my_b = lax.rem(my_d, 2)
    other_b = 1 - my_b
    mate = my_j * 2 + other_b

    def slot_of(index, parity):
        t, d = lax.div(index, nd), lax.rem(index, nd)
        u = t * owners + lax.div(d, 2)
        owner = lax.div(u, per_block)
        same = 1 - jnp.abs(lax.rem(owner, 2) - parity)
        at = same * half + lax.div(owner, 2)
        return lax.rem(d, 2) * slots + at * per_block + lax.rem(u, per_block)

    def each(low, high, act):
        def step(k, carry):
            act(k)
            return carry

        lax.fori_loop(low, high, step, 0)

    tok_in = pltpu.make_async_copy(tok, tokv, ssem.at[0])
    own_in = pltpu.make_async_copy(
        tok.at[:, pl.ds(pl.multiple_of(my_d * depth, 128), depth)],
        xbuf.at[slot_of(me, my_b)],
        ssem.at[1],
    )
    low_in = [
        pltpu.make_async_copy(ag, agv, ssem.at[2]),
        pltpu.make_async_copy(au, auv, ssem.at[3]),
    ]
    out_maps = [
        pltpu.make_async_copy(
            do.at[:, pl.ds(pl.multiple_of(my_d * width, 128), width)],
            dov.at[i * rank : (i + 1) * rank, :],
            ssem.at[4 + i],
        )
        for i in range(3)
    ]

    def cols(ref, c):
        return ref.at[:, c * chunk : (c + 1) * chunk]

    def rows_of(ref, c):
        return ref.at[c * chunk : (c + 1) * chunk, :]

    plan = (
        (wg, wgv, cols), (wu, wuv, cols), (go, gov, cols), (uo, uov, cols),
        (wd, wdv, rows_of), (di, div, cols),
    )

    def load(kind, static_c, c):
        src, dst, cut = plan[kind]
        return pltpu.make_async_copy(cut(src, static_c), dst.at[c], wsem.at[kind, c])

    tok_in.start()
    own_in.start()
    for copy in low_in:
        copy.start()
    for c in range(nc):
        for kind in range(4):
            load(kind, c, c).start()
    barrier = pltpu.get_barrier_semaphore()

    def place(index):
        return {"tensor": lax.div(index, nd), "dp": lax.rem(index, nd)}

    def greet(k):
        pl.semaphore_signal(
            barrier, inc=1, device_id=place(lax.rem(me + k, n)), device_id_type=MESH
        )

    each(1, n, greet)
    tok_in.wait()
    pl.semaphore_wait(barrier, n - 1)

    def remote(src, dst, send_sem, recv_sem, device):
        return pltpu.make_async_remote_copy(
            src_ref=src, dst_ref=dst, send_sem=send_sem, recv_sem=recv_sem,
            device_id=device, device_id_type=MESH,
        )

    def at_dp(d):
        return {"tensor": my_t, "dp": d}

    first_off = (nt // 2) * nd

    def tok_target(k):
        return lax.rem(me + first_off + k, n)

    def tok_copy(k):
        index = tok_target(k)
        d = lax.rem(index, nd)
        return remote(
            tokv.at[:, pl.ds(pl.multiple_of(d * depth, 128), depth)],
            xbuf.at[slot_of(me, lax.rem(d, 2))],
            tok_s.at[k], tok_r.at[me], place(index),
        )

    def tok_start(k):
        @pl.when(tok_target(k) != me)
        def _():
            tok_copy(k).start()

    def tok_sent(k):
        @pl.when(tok_target(k) != me)
        def _():
            tok_copy(k).wait_send()

    def tok_wait(s):
        def one(u):
            index = lax.div(u, owners) * nd + lax.rem(u, owners) * 2 + s

            @pl.when(index != me)
            def _():
                remote(
                    tokv.at[:, pl.ds(0, depth)], xbuf.at[slot_of(index, my_b)],
                    tok_s.at[0], tok_r.at[index], place(index),
                ).wait_recv()

        each(0, slots, one)

    def gather_rows(s):
        x[s] = (
            xbuf[pl.ds(s * slots, slots)].astype(jnp.float32).reshape(side, depth).astype(jnp.bfloat16)
        )

    @pl.when(my_b == 0)
    def _():
        each(0, n, tok_start)

    own_in.wait()
    tok_wait(0)

    @pl.when(my_b == 1)
    def _():
        each(0, n, tok_start)

    for c in range(nc):
        for kind in range(4, 6):
            load(kind, c, c).start()
    for copy in out_maps:
        copy.start()

    def low_at(d):
        return (1 - jnp.abs(lax.rem(d, 2) - my_b)) * half + lax.div(d, 2)

    def low_copy(s, k):
        d = lax.rem(my_d + k, nd)
        return remote(
            lowp.at[s, low_at(d)], lowr.at[s, k - 1], low_s.at[s, k - 1], low_r.at[s, k - 1],
            at_dp(d),
        )

    def low_part(s):
        @pl.when(s == 0)
        def _():
            for copy in low_in:
                copy.wait()

        for which, ref in ((0, agv), (1, auv)):
            low = dot_rows(x[s], ref[...])
            for d in range(nd):
                lowp[s, d, which] = low[d * rows : (d + 1) * rows]
        for k in range(1, nd):
            low_copy(s, k).start()

    def a_copy(q):
        return remote(send_a.at[q], recv_a.at[q], a_s.at[q], a_r.at[q], at_dp(mate))

    def ahead(k):
        return lax.rem(my_j + k, half)

    def behind(k):
        return lax.rem(my_j + half - k, half) * 2 + my_b

    def b_copy(q, k):
        return remote(
            send_b.at[q, k - 1], recv_b.at[q, k - 1],
            b_s.at[q, k - 1], b_r.at[q, k - 1], at_dp(ahead(k) * 2 + my_b),
        )

    def h_copy(q, k):
        return remote(
            hid.at[q, my_d], hid.at[q, my_d],
            h_s.at[q, k - 1], h_r.at[q, k - 1], at_dp(ahead(k) * 2 + my_b),
        )

    def p_copy(q):
        return remote(hid.at[q, my_d], hid.at[q, my_d], p_s.at[q], p_r.at[q], at_dp(mate))

    def f_copy(q, k):
        return remote(
            hid.at[q, behind(k)], hid.at[q, behind(k)],
            f_s.at[q, k - 1], f_r.at[q, k - 1], at_dp(mate),
        )

    def rows_at(j):
        return pl.ds(pl.multiple_of(j * rows, rows), rows)

    def split(q):
        return lax.div(q, nc), lax.rem(q, nc)

    def up_part(q):
        s, c = split(q)

        @pl.when(q == nc)
        def _():
            tok_wait(1)

        @pl.when(c == 0)
        def _():
            gather_rows(s)

        @pl.when(s == 0)
        def _():
            load(0, 0, c).wait()
            load(1, 0, c).wait()

        for which, ref in ((0, wgv), (1, wuv)):
            value = jnp.dot(x[s], ref[c], preferred_element_type=jnp.float32)
            send_a[q, which] = value[: side // 2].astype(jnp.bfloat16)
            part[q, which] = value[side // 2 :]
        a_copy(q).start()

        @pl.when(c == 0)
        def _():
            low_part(s)

    def pair_sum(q):
        a_copy(q).wait_recv()
        for k in range(1, half):
            at = rows_at(ahead(k))
            for which in range(2):
                send_b[q, k - 1, which] = (
                    part[q, which, at, :] + recv_a[q, which, at, :].astype(jnp.float32)
                ).astype(jnp.bfloat16)
            b_copy(q, k).start()

    def activate(q):
        s, c = split(q)

        @pl.when(c == 0)
        def _():
            for k in range(1, nd):
                low_copy(s, k).wait_recv()
            total = lowp[s, half + my_j]
            for k in range(1, nd):
                total = total + lowr[s, k - 1]
            lowb[s] = total.astype(jnp.bfloat16)

        @pl.when(s == 0)
        def _():
            load(2, 0, c).wait()
            load(3, 0, c).wait()

        for k in range(1, half):
            b_copy(q, k).wait_recv()
        sums = []
        at = rows_at(my_j)
        for which, ref in ((0, gov), (1, uov)):
            value = part[q, which, at, :] + recv_a[q, which, at, :].astype(jnp.float32)
            for k in range(1, half):
                value = value + recv_b[q, k - 1, which].astype(jnp.float32)
            value = value + adapter_scale_factor * jnp.dot(
                lowb[s, which], ref[c], preferred_element_type=jnp.float32
            )
            sums.append(value)
        gate, up = sums
        hid[q, my_d] = (gate / (1.0 + jnp.exp(-gate)) * up).astype(jnp.bfloat16)
        for k in range(1, half):
            h_copy(q, k).start()
        p_copy(q).start()

    def forward(q):
        for k in range(1, half):
            h_copy(q, k).wait_recv()
            f_copy(q, k).start()

    step = 512 if width % 512 == 0 else width

    def down_part(q):
        s, c = split(q)

        @pl.when(s == 0)
        def _():
            load(4, 0, c).wait()
            load(5, 0, c).wait()

        p_copy(q).wait_recv()
        for k in range(1, half):
            f_copy(q, k).wait_recv()
        lhs = hid[q].reshape(side, chunk)

        @pl.when(c == 0)
        def _():
            acc[s] = jnp.zeros((side, width), jnp.float32)
            dl[s] = jnp.zeros((side, dl.shape[2]), jnp.float32)

        for first in range(0, width, step):
            acc[s, :, first : first + step] += jnp.dot(
                lhs, wdv[c, :, first : first + step], preferred_element_type=jnp.float32
            )
        dl[s] += dot_rows(lhs, div[c])

        @pl.when(c == nc - 1)
        def _():
            finish(s)

    def block_at(t):
        return pl.ds(pl.multiple_of(t * block, block), block)

    def o_copy(k):
        t = lax.rem(my_t + k, nt)
        return remote(
            osend.at[k - 1], orecv.at[k - 1], o_s.at[k - 1], o_r.at[k - 1],
            {"tensor": t, "dp": my_d},
        )

    def l_target(m):
        u = lax.rem((my_t + nt // 2) * owners + m, slots)
        return u, lax.div(u, owners) * nd + lax.rem(u, owners) * 2 + 1

    def l_copy(m):
        u, index = l_target(m)
        return remote(straight.at[u], land.at[me], l_s.at[m], l_r.at[me], place(index))

    def l_start(m):
        u, index = l_target(m)

        @pl.when(index != me)
        def _():
            l_copy(m).start()

        @pl.when(index == me)
        def _():
            land[me] = straight[u]

    def l_sent(m):
        u, index = l_target(m)

        @pl.when(index != me)
        def _():
            l_copy(m).wait_send()

    def finish(s):
        @pl.when(s == 0)
        def _():
            for copy in out_maps:
                copy.wait()

        low = dl[s]
        high = low.astype(jnp.bfloat16)
        rest = low - high.astype(jnp.float32)
        middle = rest.astype(jnp.bfloat16)
        last = (rest - middle.astype(jnp.float32)).astype(jnp.bfloat16)
        terms = jnp.concatenate([high, middle, last], axis=1)
        for first in range(0, width, step):
            acc[s, :, first : first + step] += adapter_scale_factor * jnp.dot(
                terms, dov[:, first : first + step], preferred_element_type=jnp.float32
            )

        @pl.when(s == 0)
        def _():
            def o_send(k):
                osend[k - 1] = acc[0, block_at(lax.rem(my_t + k, nt)), :].astype(jnp.bfloat16)
                o_copy(k).start()

            each(1, nt, o_send)

        @pl.when(s == 1)
        def _():
            straight[...] = acc[1].reshape(slots, tok_dev, width).astype(jnp.bfloat16)
            each(0, slots, l_start)

    mine = pl.ds(pl.multiple_of(my_d * width, 128), width)

    def z_copy(i):
        return remote(fin.at[i], out.at[:, mine], z_s.at[i], z_r.at[my_d], at_dp(2 * i))

    stages = ((up_part, 0), (pair_sum, SUM_LAG), (activate, ACT_LAG), (forward, FWD_LAG), (down_part, DOWN_LAG))

    def turn(i, carry):
        for stage, lag in stages:
            q = i - lag
            pl.when(jnp.logical_and(q >= 0, q < items))(functools.partial(stage, q))
        return carry

    lax.fori_loop(0, items + DOWN_LAG, turn, 0)

    def o_take(k):
        o_copy(k).wait_recv()
        acc[0, block_at(my_t), :] += orecv[k - 1].astype(jnp.float32)

    each(1, nt, o_take)
    fin[...] = acc[0, block_at(my_t), :].reshape(owners, tok_dev, width).astype(jnp.bfloat16)
    for i in range(owners):
        @pl.when(my_d != 2 * i)
        def _():
            z_copy(i).start()

        @pl.when(my_d == 2 * i)
        def _():
            out[:, mine] = fin[i]

    @pl.when(my_b == 1)
    def _():
        def l_wait(index):
            @pl.when(index != me)
            def _():
                remote(
                    straight.at[0], land.at[index], l_s.at[0], l_r.at[index], place(index)
                ).wait_recv()

        each(0, n, l_wait)
        for d in range(nd):
            total = land[d].astype(jnp.float32)
            for t in range(1, nt):
                total = total + land[t * nd + d].astype(jnp.float32)
            out[:, d * width : (d + 1) * width] = total.astype(jnp.bfloat16)

    each(0, n, tok_sent)
    for s in range(HALVES):
        for k in range(1, nd):
            low_copy(s, k).wait_send()

    def drain(q):
        a_copy(q).wait_send()
        p_copy(q).wait_send()
        for k in range(1, half):
            b_copy(q, k).wait_send()
            h_copy(q, k).wait_send()
            f_copy(q, k).wait_send()

    each(0, items, drain)
    each(1, nt, lambda k: o_copy(k).wait_send())
    each(0, slots, l_sent)

    for i in range(owners):
        @pl.when(my_d != 2 * i)
        def _():
            z_copy(i).wait_send()

    @pl.when(my_b == 0)
    def _():
        def z_wait(d):
            @pl.when(d != my_d)
            def _():
                place_of = pl.ds(pl.multiple_of(d * width, 128), width)
                remote(fin.at[0], out.at[:, place_of], z_s.at[0], z_r.at[d], at_dp(d)).wait_recv()

        each(0, nd, z_wait)


def body(tok, wg, wu, wd, ag, go, au, uo, di, do):
    nt = lax.axis_size("tensor")
    nd = lax.axis_size("dp")
    n = nt * nd
    half = nd // 2
    tok_dev = tok.shape[0]
    depth, hidden = wg.shape
    width = wd.shape[1]
    rank = ag.shape[1]
    chunk = 512 if hidden % 512 == 0 else hidden
    nc = hidden // chunk
    total = n * tok_dev
    side = total // HALVES
    rows = side // nd
    owners = nd // HALVES
    block = owners * tok_dev
    items = HALVES * nc
    far = half - 1
    bf, f32 = jnp.bfloat16, jnp.float32
    vm, dma = pltpu.VMEM, pltpu.SemaphoreType.DMA
    scratch = [
        vm((tok_dev, depth * nd), bf), vm((n, tok_dev, depth), bf), vm((HALVES, side, depth), bf),
        vm((nc, depth, chunk), bf), vm((nc, depth, chunk), bf), vm((nc, chunk, width), bf),
        vm((rank, depth), bf), vm((rank, depth), bf),
        vm((nc, rank, chunk), bf), vm((nc, rank, chunk), bf), vm((nc, rank, chunk), bf),
        vm((3 * rank, width), bf),
        vm((HALVES, nd, 2, rows, rank), f32), vm((HALVES, nd - 1, 2, rows, rank), f32),
        vm((HALVES, 2, rows, rank), bf),
        vm((items, 2, side // 2, chunk), f32),
        vm((items, 2, side // 2, chunk), bf), vm((items, 2, side // 2, chunk), bf),
        vm((items, far, 2, rows, chunk), bf), vm((items, far, 2, rows, chunk), bf),
        vm((items, nd, rows, chunk), bf),
        vm((HALVES, side, width), f32), vm((HALVES, side, rank), f32),
        vm((nt - 1, block, width), bf), vm((nt - 1, block, width), bf),
        vm((owners, tok_dev, width), bf),
        vm((nt * owners, tok_dev, width), bf), vm((n, tok_dev, width), bf),
        dma((6, nc)), dma((7,)), dma((n,)), dma((n,)),
        dma((HALVES, nd - 1)), dma((HALVES, nd - 1)),
        dma((items,)), dma((items,)), dma((items, far)), dma((items, far)),
        dma((items, far)), dma((items, far)), dma((items,)), dma((items,)),
        dma((items, far)), dma((items, far)),
        dma((nt - 1,)), dma((nt - 1,)), dma((owners,)), dma((nd,)),
        dma((nt * owners,)), dma((n,)),
    ]
    return pl.pallas_call(
        functools.partial(kernel, nt, nd, nc),
        out_shape=jax.ShapeDtypeStruct((tok_dev, width * nd), bf),
        in_specs=[pl.BlockSpec(memory_space=pl.ANY)] * 10,
        out_specs=pl.BlockSpec(memory_space=pltpu.VMEM),
        scratch_shapes=scratch,
        compiler_params=pltpu.CompilerParams(
            collective_id=0, has_side_effects=True, vmem_limit_bytes=67043328
        ),
    )(tok, wg, wu, wd, ag.T, go, au.T, uo, di.T, do)


def solution(mesh):
    placed = (
        P(("groups", "tensor", "dp"), None),
        P("dp", "tensor"),
        P("dp", "tensor"),
        P("tensor", "dp"),
        P(("groups", "dp"), None),
        P(None, ("groups", "tensor")),
        P(("groups", "dp"), None),
        P(None, ("groups", "tensor")),
        P(("groups", "tensor"), None),
        P(None, "groups"),
    )
    return jax.shard_map(
        body,
        mesh=mesh,
        in_specs=placed,
        out_specs=P(("groups", "tensor", "dp"), None),
        check_vma=False,
    )
```

```python
import functools

import jax
import jax.numpy as jnp
from jax import lax
from jax.experimental import pallas as pl
from jax.experimental.pallas import tpu as pltpu
from jax.sharding import PartitionSpec as P

adapter_scale_factor = 0.5
MESH = pl.DeviceIdType.MESH
HALVES = 2
EARLY = 2
SUM_LAG, ACT_LAG, FWD_LAG, DOWN_LAG = 1, 4, 7, 9


def dot_rows(a, b):
    return lax.dot_general(a, b, (((1,), (1,)), ((), ())), preferred_element_type=jnp.float32)


def kernel(
    nt, nd, nc,
    tok, wg, wu, wd, ag, go, au, uo, di, do, out,
    tokv, xbuf, x, wgv, wuv, wdv, agv, auv, gov, uov, div, dov,
    lowp, lowr, added, part, send_a, recv_a, send_b, recv_b, hid, acc, dl,
    osend, orecv, fin, straight, land,
    wsem, ssem, tok_s, tok_r, low_s, low_r, a_s, a_r, b_s, b_r,
    h_s, h_r, p_s, p_r, f_s, f_r, o_s, o_r, z_s, z_r, l_s, l_r,
):
    n = nt * nd
    half = nd // 2
    depth = wg.shape[0]
    chunk = wgv.shape[2]
    width = wd.shape[1]
    rank = agv.shape[0]
    tok_dev = tok.shape[0]
    total_rows = n * tok_dev
    side = total_rows // HALVES
    rows = side // nd
    owners = nd // HALVES
    block = owners * tok_dev
    slots = nt * owners
    per_block = slots // nd
    items = HALVES * nc
    my_t = lax.axis_index("tensor")
    my_d = lax.axis_index("dp")
    me = my_t * nd + my_d
    my_j = lax.div(my_d, 2)
    my_b = lax.rem(my_d, 2)
    other_b = 1 - my_b
    mate = my_j * 2 + other_b

    def slot_of(index, parity):
        t, d = lax.div(index, nd), lax.rem(index, nd)
        u = t * owners + lax.div(d, 2)
        owner = lax.div(u, per_block)
        same = 1 - jnp.abs(lax.rem(owner, 2) - parity)
        at = same * half + lax.div(owner, 2)
        return lax.rem(d, 2) * slots + at * per_block + lax.rem(u, per_block)

    def each(low, high, act):
        def step(k, carry):
            act(k)
            return carry

        lax.fori_loop(low, high, step, 0)

    tok_in = pltpu.make_async_copy(tok, tokv, ssem.at[0])
    own_in = pltpu.make_async_copy(
        tok.at[:, pl.ds(pl.multiple_of(my_d * depth, 128), depth)],
        xbuf.at[slot_of(me, my_b)],
        ssem.at[1],
    )
    low_in = [
        pltpu.make_async_copy(ag, agv, ssem.at[2]),
        pltpu.make_async_copy(au, auv, ssem.at[3]),
    ]
    out_maps = [
        pltpu.make_async_copy(
            do.at[:, pl.ds(pl.multiple_of(my_d * width, 128), width)],
            dov.at[i * rank : (i + 1) * rank, :],
            ssem.at[4 + i],
        )
        for i in range(3)
    ]

    def cols(ref, c):
        return ref.at[:, c * chunk : (c + 1) * chunk]

    def rows_of(ref, c):
        return ref.at[c * chunk : (c + 1) * chunk, :]

    plan = (
        (wg, wgv, cols), (wu, wuv, cols), (go, gov, cols), (uo, uov, cols),
        (wd, wdv, rows_of), (di, div, cols),
    )

    def load(kind, static_c, c):
        src, dst, cut = plan[kind]
        return pltpu.make_async_copy(cut(src, static_c), dst.at[c], wsem.at[kind, c])

    tok_in.start()
    own_in.start()
    for copy in low_in:
        copy.start()
    early = min(EARLY, nc)

    def load_up(low, high):
        for c in range(low, high):
            for kind in range(4):
                load(kind, c, c).start()

    load_up(0, early)
    barrier = pltpu.get_barrier_semaphore()

    def place(index):
        return {"tensor": lax.div(index, nd), "dp": lax.rem(index, nd)}

    def greet(k):
        pl.semaphore_signal(
            barrier, inc=1, device_id=place(lax.rem(me + k, n)), device_id_type=MESH
        )

    each(1, n, greet)
    tok_in.wait()
    pl.semaphore_wait(barrier, n - 1)

    def remote(src, dst, send_sem, recv_sem, device):
        return pltpu.make_async_remote_copy(
            src_ref=src, dst_ref=dst, send_sem=send_sem, recv_sem=recv_sem,
            device_id=device, device_id_type=MESH,
        )

    def at_dp(d):
        return {"tensor": my_t, "dp": d}

    first_off = (nt // 2) * nd

    def tok_target(k):
        return lax.rem(me + first_off + k, n)

    def tok_copy(k):
        index = tok_target(k)
        d = lax.rem(index, nd)
        return remote(
            tokv.at[:, pl.ds(pl.multiple_of(d * depth, 128), depth)],
            xbuf.at[slot_of(me, lax.rem(d, 2))],
            tok_s.at[k], tok_r.at[me], place(index),
        )

    def tok_start(k):
        @pl.when(tok_target(k) != me)
        def _():
            tok_copy(k).start()

    def tok_sent(k):
        @pl.when(tok_target(k) != me)
        def _():
            tok_copy(k).wait_send()

    def tok_wait(s):
        def one(u):
            index = lax.div(u, owners) * nd + lax.rem(u, owners) * 2 + s

            @pl.when(index != me)
            def _():
                remote(
                    tokv.at[:, pl.ds(0, depth)], xbuf.at[slot_of(index, my_b)],
                    tok_s.at[0], tok_r.at[index], place(index),
                ).wait_recv()

        each(0, slots, one)

    def gather_rows(s):
        x[s] = (
            xbuf[pl.ds(s * slots, slots)].astype(jnp.float32).reshape(side, depth).astype(jnp.bfloat16)
        )

    @pl.when(my_b == 0)
    def _():
        each(0, n, tok_start)

    load_up(early, nc)

    own_in.wait()
    tok_wait(0)

    @pl.when(my_b == 1)
    def _():
        each(0, n, tok_start)

    for c in range(nc):
        for kind in range(4, 6):
            load(kind, c, c).start()
    for copy in out_maps:
        copy.start()

    def low_at(d):
        return (1 - jnp.abs(lax.rem(d, 2) - my_b)) * half + lax.div(d, 2)

    def low_copy(s, k):
        d = lax.rem(my_d + k, nd)
        return remote(
            lowp.at[s, low_at(d)], lowr.at[s, k - 1], low_s.at[s, k - 1], low_r.at[s, k - 1],
            at_dp(d),
        )

    def low_part(s):
        @pl.when(s == 0)
        def _():
            for copy in low_in:
                copy.wait()

        for which, ref in ((0, agv), (1, auv)):
            low = dot_rows(x[s], ref[...])
            for d in range(nd):
                lowp[s, d, which] = low[d * rows : (d + 1) * rows]
        for k in range(1, nd):
            low_copy(s, k).start()

    def a_copy(q):
        return remote(send_a.at[q], recv_a.at[q], a_s.at[q], a_r.at[q], at_dp(mate))

    def ahead(k):
        return lax.rem(my_j + k, half)

    def behind(k):
        return lax.rem(my_j + half - k, half) * 2 + my_b

    def b_copy(q, k):
        return remote(
            send_b.at[q, k - 1], recv_b.at[q, k - 1],
            b_s.at[q, k - 1], b_r.at[q, k - 1], at_dp(ahead(k) * 2 + my_b),
        )

    def h_copy(q, k):
        return remote(
            hid.at[q, my_d], hid.at[q, my_d],
            h_s.at[q, k - 1], h_r.at[q, k - 1], at_dp(ahead(k) * 2 + my_b),
        )

    def p_copy(q):
        return remote(hid.at[q, my_d], hid.at[q, my_d], p_s.at[q], p_r.at[q], at_dp(mate))

    def f_copy(q, k):
        return remote(
            hid.at[q, behind(k)], hid.at[q, behind(k)],
            f_s.at[q, k - 1], f_r.at[q, k - 1], at_dp(mate),
        )

    def rows_at(j):
        return pl.ds(pl.multiple_of(j * rows, rows), rows)

    def split(q):
        return lax.div(q, nc), lax.rem(q, nc)

    piece = 128 if chunk % 128 == 0 else chunk

    def up_part(q):
        s, c = split(q)

        @pl.when(q == nc)
        def _():
            tok_wait(1)

        @pl.when(c == 0)
        def _():
            gather_rows(s)

        @pl.when(s == 0)
        def _():
            load(0, 0, c).wait()
            load(1, 0, c).wait()

        for which, ref in ((0, wgv), (1, wuv)):
            for first in range(0, chunk, piece):
                at = slice(first, first + piece)
                value = jnp.dot(x[s], ref[c, :, at], preferred_element_type=jnp.float32)
                send_a[q, which, :, at] = value[: side // 2].astype(jnp.bfloat16)
                part[q, which, :, at] = value[side // 2 :]
        a_copy(q).start()

        @pl.when(c == 0)
        def _():
            low_part(s)

    def pair_sum(q):
        a_copy(q).wait_recv()
        for k in range(1, half):
            at = rows_at(ahead(k))
            for which in range(2):
                send_b[q, k - 1, which] = (
                    part[q, which, at, :] + recv_a[q, which, at, :].astype(jnp.float32)
                ).astype(jnp.bfloat16)
            b_copy(q, k).start()

    def activate(q):
        s, c = split(q)

        @pl.when(c == 0)
        def _():
            for k in range(1, nd):
                low_copy(s, k).wait_recv()

            @pl.when(s == 0)
            def _():
                for at in range(nc):
                    load(2, at, at).wait()
                    load(3, at, at).wait()

            total = lowp[s, half + my_j]
            for k in range(1, nd):
                total = total + lowr[s, k - 1]
            low = total.astype(jnp.bfloat16)
            for which, ref in ((0, gov), (1, uov)):
                for at in range(nc):
                    added[s, which, at] = adapter_scale_factor * jnp.dot(
                        low[which], ref[at], preferred_element_type=jnp.float32
                    )

        for k in range(1, half):
            b_copy(q, k).wait_recv()
        sums = []
        at = rows_at(my_j)
        for which in range(2):
            value = added[s, which, c] + part[q, which, at, :] + recv_a[q, which, at, :].astype(jnp.float32)
            for k in range(1, half):
                value = value + recv_b[q, k - 1, which].astype(jnp.float32)
            sums.append(value)
        gate, up = sums
        hid[q, my_d] = (gate / (1.0 + jnp.exp(-gate)) * up).astype(jnp.bfloat16)
        for k in range(1, half):
            h_copy(q, k).start()
        p_copy(q).start()

    def forward(q):
        for k in range(1, half):
            h_copy(q, k).wait_recv()
            f_copy(q, k).start()

    step = 512 if width % 512 == 0 else width

    def down_part(q):
        s, c = split(q)

        @pl.when(s == 0)
        def _():
            load(4, 0, c).wait()
            load(5, 0, c).wait()

        p_copy(q).wait_recv()
        for k in range(1, half):
            f_copy(q, k).wait_recv()
        lhs = hid[q].reshape(side, chunk)

        @pl.when(c == 0)
        def _():
            acc[s] = jnp.zeros((side, width), jnp.float32)
            dl[s] = jnp.zeros((side, dl.shape[2]), jnp.float32)

        for first in range(0, width, step):
            acc[s, :, first : first + step] += jnp.dot(
                lhs, wdv[c, :, first : first + step], preferred_element_type=jnp.float32
            )
        dl[s] += dot_rows(lhs, div[c])

        @pl.when(c == nc - 1)
        def _():
            finish(s)

    def block_at(t):
        return pl.ds(pl.multiple_of(t * block, block), block)

    def o_copy(k):
        t = lax.rem(my_t + k, nt)
        return remote(
            osend.at[k - 1], orecv.at[k - 1], o_s.at[k - 1], o_r.at[k - 1],
            {"tensor": t, "dp": my_d},
        )

    def l_target(m):
        u = lax.rem((my_t + nt // 2) * owners + m, slots)
        return u, lax.div(u, owners) * nd + lax.rem(u, owners) * 2 + 1

    def l_copy(m):
        u, index = l_target(m)
        return remote(straight.at[u], land.at[me], l_s.at[m], l_r.at[me], place(index))

    def l_start(m):
        u, index = l_target(m)

        @pl.when(index != me)
        def _():
            l_copy(m).start()

        @pl.when(index == me)
        def _():
            land[me] = straight[u]

    def l_sent(m):
        u, index = l_target(m)

        @pl.when(index != me)
        def _():
            l_copy(m).wait_send()

    def finish(s):
        @pl.when(s == 0)
        def _():
            for copy in out_maps:
                copy.wait()

        low = dl[s]
        high = low.astype(jnp.bfloat16)
        rest = low - high.astype(jnp.float32)
        middle = rest.astype(jnp.bfloat16)
        last = (rest - middle.astype(jnp.float32)).astype(jnp.bfloat16)
        terms = jnp.concatenate([high, middle, last], axis=1)
        for first in range(0, width, step):
            acc[s, :, first : first + step] += adapter_scale_factor * jnp.dot(
                terms, dov[:, first : first + step], preferred_element_type=jnp.float32
            )

        @pl.when(s == 0)
        def _():
            def o_send(k):
                osend[k - 1] = acc[0, block_at(lax.rem(my_t + k, nt)), :].astype(jnp.bfloat16)
                o_copy(k).start()

            each(1, nt, o_send)

        @pl.when(s == 1)
        def _():
            straight[...] = acc[1].reshape(slots, tok_dev, width).astype(jnp.bfloat16)
            each(0, slots, l_start)

    mine = pl.ds(pl.multiple_of(my_d * width, 128), width)

    def z_copy(i):
        return remote(fin.at[i], out.at[:, mine], z_s.at[i], z_r.at[my_d], at_dp(2 * i))

    stages = ((up_part, 0), (pair_sum, SUM_LAG), (activate, ACT_LAG), (forward, FWD_LAG), (down_part, DOWN_LAG))

    def turn(i, carry):
        for stage, lag in stages:
            q = i - lag
            pl.when(jnp.logical_and(q >= 0, q < items))(functools.partial(stage, q))
        return carry

    lax.fori_loop(0, items + DOWN_LAG, turn, 0)

    def o_take(k):
        o_copy(k).wait_recv()
        acc[0, block_at(my_t), :] += orecv[k - 1].astype(jnp.float32)

    each(1, nt, o_take)
    fin[...] = acc[0, block_at(my_t), :].reshape(owners, tok_dev, width).astype(jnp.bfloat16)
    for i in range(owners):
        @pl.when(my_d != 2 * i)
        def _():
            z_copy(i).start()

        @pl.when(my_d == 2 * i)
        def _():
            out[:, mine] = fin[i]

    each(0, n, tok_sent)
    for s in range(HALVES):
        for k in range(1, nd):
            low_copy(s, k).wait_send()

    def drain(q):
        a_copy(q).wait_send()
        p_copy(q).wait_send()
        for k in range(1, half):
            b_copy(q, k).wait_send()
            h_copy(q, k).wait_send()
            f_copy(q, k).wait_send()

    each(0, items, drain)
    @pl.when(my_b == 1)
    def _():
        def l_wait(index):
            @pl.when(index != me)
            def _():
                remote(
                    straight.at[0], land.at[index], l_s.at[0], l_r.at[index], place(index)
                ).wait_recv()

        each(0, n, l_wait)
        for d in range(nd):
            total = land[d].astype(jnp.float32)
            for t in range(1, nt):
                total = total + land[t * nd + d].astype(jnp.float32)
            out[:, d * width : (d + 1) * width] = total.astype(jnp.bfloat16)

    each(1, nt, lambda k: o_copy(k).wait_send())
    each(0, slots, l_sent)

    for i in range(owners):
        @pl.when(my_d != 2 * i)
        def _():
            z_copy(i).wait_send()

    @pl.when(my_b == 0)
    def _():
        def z_wait(d):
            @pl.when(d != my_d)
            def _():
                place_of = pl.ds(pl.multiple_of(d * width, 128), width)
                remote(fin.at[0], out.at[:, place_of], z_s.at[0], z_r.at[d], at_dp(d)).wait_recv()

        each(0, nd, z_wait)


def body(tok, wg, wu, wd, ag, go, au, uo, di, do):
    nt = lax.axis_size("tensor")
    nd = lax.axis_size("dp")
    n = nt * nd
    half = nd // 2
    tok_dev = tok.shape[0]
    depth, hidden = wg.shape
    width = wd.shape[1]
    rank = ag.shape[1]
    chunk = 512 if hidden % 512 == 0 else hidden
    nc = hidden // chunk
    total = n * tok_dev
    side = total // HALVES
    rows = side // nd
    owners = nd // HALVES
    block = owners * tok_dev
    items = HALVES * nc
    far = half - 1
    bf, f32 = jnp.bfloat16, jnp.float32
    vm, dma = pltpu.VMEM, pltpu.SemaphoreType.DMA
    scratch = [
        vm((tok_dev, depth * nd), bf), vm((n, tok_dev, depth), bf), vm((HALVES, side, depth), bf),
        vm((nc, depth, chunk), bf), vm((nc, depth, chunk), bf), vm((nc, chunk, width), bf),
        vm((rank, depth), bf), vm((rank, depth), bf),
        vm((nc, rank, chunk), bf), vm((nc, rank, chunk), bf), vm((nc, rank, chunk), bf),
        vm((3 * rank, width), bf),
        vm((HALVES, nd, 2, rows, rank), f32), vm((HALVES, nd - 1, 2, rows, rank), f32),
        vm((HALVES, 2, nc, rows, chunk), f32),
        vm((items, 2, side // 2, chunk), f32),
        vm((items, 2, side // 2, chunk), bf), vm((items, 2, side // 2, chunk), bf),
        vm((items, far, 2, rows, chunk), bf), vm((items, far, 2, rows, chunk), bf),
        vm((items, nd, rows, chunk), bf),
        vm((HALVES, side, width), f32), vm((HALVES, side, rank), f32),
        vm((nt - 1, block, width), bf), vm((nt - 1, block, width), bf),
        vm((owners, tok_dev, width), bf),
        vm((nt * owners, tok_dev, width), bf), vm((n, tok_dev, width), bf),
        dma((6, nc)), dma((7,)), dma((n,)), dma((n,)),
        dma((HALVES, nd - 1)), dma((HALVES, nd - 1)),
        dma((items,)), dma((items,)), dma((items, far)), dma((items, far)),
        dma((items, far)), dma((items, far)), dma((items,)), dma((items,)),
        dma((items, far)), dma((items, far)),
        dma((nt - 1,)), dma((nt - 1,)), dma((owners,)), dma((nd,)),
        dma((nt * owners,)), dma((n,)),
    ]
    return pl.pallas_call(
        functools.partial(kernel, nt, nd, nc),
        out_shape=jax.ShapeDtypeStruct((tok_dev, width * nd), bf),
        in_specs=[pl.BlockSpec(memory_space=pl.ANY)] * 10,
        out_specs=pl.BlockSpec(memory_space=pltpu.VMEM),
        scratch_shapes=scratch,
        compiler_params=pltpu.CompilerParams(
            collective_id=0, has_side_effects=True, vmem_limit_bytes=67043328
        ),
    )(tok, wg, wu, wd, ag.T, go, au.T, uo, di.T, do)


def solution(mesh):
    placed = (
        P(("groups", "tensor", "dp"), None),
        P("dp", "tensor"),
        P("dp", "tensor"),
        P("tensor", "dp"),
        P(("groups", "dp"), None),
        P(None, ("groups", "tensor")),
        P(("groups", "dp"), None),
        P(None, ("groups", "tensor")),
        P(("groups", "tensor"), None),
        P(None, "groups"),
    )
    return jax.shard_map(
        body,
        mesh=mesh,
        in_specs=placed,
        out_specs=P(("groups", "tensor", "dp"), None),
        check_vma=False,
    )
```

```python
import functools

import jax
import jax.numpy as jnp
from jax import lax
from jax.experimental import pallas as pl
from jax.experimental.pallas import tpu as pltpu
from jax.sharding import PartitionSpec as P

adapter_scale_factor = 0.5
MESH = pl.DeviceIdType.MESH
HALVES = 2
EARLY = 1
FIRST_LAGS = (0, 1, 5, 9, 12)
SECOND_LAGS = (0, 2, 5, 9, 12)
GAP = 0


def dot_rows(a, b):
    return lax.dot_general(a, b, (((1,), (1,)), ((), ())), preferred_element_type=jnp.float32)


def kernel(
    nt, nd, nc,
    tok, wg, wu, wd, ag, go, au, uo, di, do, out,
    tokv, xbuf, x, wgv, wuv, wdv, agv, auv, gov, uov, div, dov,
    lowp, lowr, added, part, send_a, recv_a, send_b, recv_b, hid, acc, dl,
    osend, orecv, fin, straight, land,
    wsem, ssem, tok_s, tok_r, low_s, low_r, a_s, a_r, b_s, b_r,
    h_s, h_r, p_s, p_r, f_s, f_r, o_s, o_r, z_s, z_r, l_s, l_r,
):
    n = nt * nd
    half = nd // 2
    depth = wg.shape[0]
    chunk = wgv.shape[2]
    width = wd.shape[1]
    rank = agv.shape[0]
    tok_dev = tok.shape[0]
    total_rows = n * tok_dev
    side = total_rows // HALVES
    rows = side // nd
    owners = nd // HALVES
    block = owners * tok_dev
    slots = nt * owners
    per_block = slots // nd
    items = HALVES * nc
    my_t = lax.axis_index("tensor")
    my_d = lax.axis_index("dp")
    me = my_t * nd + my_d
    my_j = lax.div(my_d, 2)
    my_b = lax.rem(my_d, 2)
    other_b = 1 - my_b
    mate = my_j * 2 + other_b

    def slot_of(index, parity):
        t, d = lax.div(index, nd), lax.rem(index, nd)
        u = t * owners + lax.div(d, 2)
        owner = lax.div(u, per_block)
        same = 1 - jnp.abs(lax.rem(owner, 2) - parity)
        at = same * half + lax.div(owner, 2)
        return lax.rem(d, 2) * slots + at * per_block + lax.rem(u, per_block)

    def each(low, high, act):
        def step(k, carry):
            act(k)
            return carry

        lax.fori_loop(low, high, step, 0)

    tok_in = pltpu.make_async_copy(tok, tokv, ssem.at[0])
    own_in = pltpu.make_async_copy(
        tok.at[:, pl.ds(pl.multiple_of(my_d * depth, 128), depth)],
        xbuf.at[slot_of(me, my_b)],
        ssem.at[1],
    )
    low_in = [
        pltpu.make_async_copy(ag, agv, ssem.at[2]),
        pltpu.make_async_copy(au, auv, ssem.at[3]),
    ]
    out_maps = [
        pltpu.make_async_copy(
            do.at[:, pl.ds(pl.multiple_of(my_d * width, 128), width)],
            dov.at[i * rank : (i + 1) * rank, :],
            ssem.at[4 + i],
        )
        for i in range(3)
    ]

    def cols(ref, c):
        return ref.at[:, c * chunk : (c + 1) * chunk]

    def rows_of(ref, c):
        return ref.at[c * chunk : (c + 1) * chunk, :]

    plan = (
        (wg, wgv, cols), (wu, wuv, cols), (go, gov, cols), (uo, uov, cols),
        (wd, wdv, rows_of), (di, div, cols),
    )

    def load(kind, static_c, c):
        src, dst, cut = plan[kind]
        return pltpu.make_async_copy(cut(src, static_c), dst.at[c], wsem.at[kind, c])

    tok_in.start()
    own_in.start()
    for copy in low_in:
        copy.start()
    early = min(EARLY, nc)

    def load_up(low, high):
        for c in range(low, high):
            for kind in range(4):
                load(kind, c, c).start()

    load_up(0, early)
    barrier = pltpu.get_barrier_semaphore()

    def place(index):
        return {"tensor": lax.div(index, nd), "dp": lax.rem(index, nd)}

    def greet(k):
        pl.semaphore_signal(
            barrier, inc=1, device_id=place(lax.rem(me + k, n)), device_id_type=MESH
        )

    each(1, n, greet)
    tok_in.wait()
    pl.semaphore_wait(barrier, n - 1)

    def remote(src, dst, send_sem, recv_sem, device):
        return pltpu.make_async_remote_copy(
            src_ref=src, dst_ref=dst, send_sem=send_sem, recv_sem=recv_sem,
            device_id=device, device_id_type=MESH,
        )

    def at_dp(d):
        return {"tensor": my_t, "dp": d}

    first_off = (nt // 2) * nd

    def tok_target(k):
        return lax.rem(me + first_off + k, n)

    def tok_copy(k):
        index = tok_target(k)
        d = lax.rem(index, nd)
        return remote(
            tokv.at[:, pl.ds(pl.multiple_of(d * depth, 128), depth)],
            xbuf.at[slot_of(me, lax.rem(d, 2))],
            tok_s.at[k], tok_r.at[me], place(index),
        )

    def tok_start(k):
        @pl.when(tok_target(k) != me)
        def _():
            tok_copy(k).start()

    def tok_sent(k):
        @pl.when(tok_target(k) != me)
        def _():
            tok_copy(k).wait_send()

    def tok_wait(s):
        def one(u):
            index = lax.div(u, owners) * nd + lax.rem(u, owners) * 2 + s

            @pl.when(index != me)
            def _():
                remote(
                    tokv.at[:, pl.ds(0, depth)], xbuf.at[slot_of(index, my_b)],
                    tok_s.at[0], tok_r.at[index], place(index),
                ).wait_recv()

        each(0, slots, one)

    def gather_rows(s):
        x[s] = (
            xbuf[pl.ds(s * slots, slots)].astype(jnp.float32).reshape(side, depth).astype(jnp.bfloat16)
        )

    @pl.when(my_b == 0)
    def _():
        each(0, n, tok_start)

    load_up(early, nc)

    own_in.wait()
    tok_wait(0)

    @pl.when(my_b == 1)
    def _():
        each(0, n, tok_start)

    for c in range(nc):
        for kind in range(4, 6):
            load(kind, c, c).start()
    for copy in out_maps:
        copy.start()

    def low_at(d):
        return (1 - jnp.abs(lax.rem(d, 2) - my_b)) * half + lax.div(d, 2)

    def low_copy(s, k):
        d = lax.rem(my_d + k, nd)
        return remote(
            lowp.at[s, low_at(d)], lowr.at[s, k - 1], low_s.at[s, k - 1], low_r.at[s, k - 1],
            at_dp(d),
        )

    def low_part(s):
        @pl.when(s == 0)
        def _():
            for copy in low_in:
                copy.wait()

        for which, ref in ((0, agv), (1, auv)):
            low = dot_rows(x[s], ref[...])
            for d in range(nd):
                lowp[s, d, which] = low[d * rows : (d + 1) * rows]
        for k in range(1, nd):
            low_copy(s, k).start()

    def a_copy(q):
        return remote(send_a.at[q], recv_a.at[q], a_s.at[q], a_r.at[q], at_dp(mate))

    def ahead(k):
        return lax.rem(my_j + k, half)

    def behind(k):
        return lax.rem(my_j + half - k, half) * 2 + my_b

    def b_copy(q, k):
        return remote(
            send_b.at[q, k - 1], recv_b.at[q, k - 1],
            b_s.at[q, k - 1], b_r.at[q, k - 1], at_dp(ahead(k) * 2 + my_b),
        )

    def h_copy(q, k):
        return remote(
            hid.at[q, my_d], hid.at[q, my_d],
            h_s.at[q, k - 1], h_r.at[q, k - 1], at_dp(ahead(k) * 2 + my_b),
        )

    def p_copy(q):
        return remote(hid.at[q, my_d], hid.at[q, my_d], p_s.at[q], p_r.at[q], at_dp(mate))

    def f_copy(q, k):
        return remote(
            hid.at[q, behind(k)], hid.at[q, behind(k)],
            f_s.at[q, k - 1], f_r.at[q, k - 1], at_dp(mate),
        )

    def rows_at(j):
        return pl.ds(pl.multiple_of(j * rows, rows), rows)

    def split(q):
        return lax.div(q, nc), lax.rem(q, nc)

    piece = 128 if chunk % 128 == 0 else chunk

    def up_part(q):
        s, c = split(q)

        @pl.when(q == nc)
        def _():
            tok_wait(1)

        @pl.when(c == 0)
        def _():
            gather_rows(s)

        @pl.when(s == 0)
        def _():
            load(0, 0, c).wait()
            load(1, 0, c).wait()

        for which, ref in ((0, wgv), (1, wuv)):
            for first in range(0, chunk, piece):
                at = slice(first, first + piece)
                value = jnp.dot(x[s], ref[c, :, at], preferred_element_type=jnp.float32)
                send_a[q, which, :, at] = value[: side // 2].astype(jnp.bfloat16)
                part[q, which, :, at] = value[side // 2 :]
        a_copy(q).start()

        @pl.when(c == 0)
        def _():
            low_part(s)

    def pair_sum(q):
        a_copy(q).wait_recv()
        for k in range(1, half):
            at = rows_at(ahead(k))
            for which in range(2):
                send_b[q, k - 1, which] = (
                    part[q, which, at, :] + recv_a[q, which, at, :].astype(jnp.float32)
                ).astype(jnp.bfloat16)
            b_copy(q, k).start()

    def activate(q):
        s, c = split(q)

        @pl.when(c == 0)
        def _():
            for k in range(1, nd):
                low_copy(s, k).wait_recv()

            @pl.when(s == 0)
            def _():
                for at in range(nc):
                    load(2, at, at).wait()
                    load(3, at, at).wait()

            total = lowp[s, half + my_j]
            for k in range(1, nd):
                total = total + lowr[s, k - 1]
            low = total.astype(jnp.bfloat16)
            for which, ref in ((0, gov), (1, uov)):
                for at in range(nc):
                    added[s, which, at] = adapter_scale_factor * jnp.dot(
                        low[which], ref[at], preferred_element_type=jnp.float32
                    )

        for k in range(1, half):
            b_copy(q, k).wait_recv()
        sums = []
        at = rows_at(my_j)
        for which in range(2):
            value = added[s, which, c] + part[q, which, at, :] + recv_a[q, which, at, :].astype(jnp.float32)
            for k in range(1, half):
                value = value + recv_b[q, k - 1, which].astype(jnp.float32)
            sums.append(value)
        gate, up = sums
        hid[q, my_d] = (gate / (1.0 + jnp.exp(-gate)) * up).astype(jnp.bfloat16)
        for k in range(1, half):
            h_copy(q, k).start()
        p_copy(q).start()

    def forward(q):
        for k in range(1, half):
            h_copy(q, k).wait_recv()
            f_copy(q, k).start()

    step = 512 if width % 512 == 0 else width

    def down_part(q):
        s, c = split(q)

        @pl.when(s == 0)
        def _():
            load(4, 0, c).wait()
            load(5, 0, c).wait()

        p_copy(q).wait_recv()
        for k in range(1, half):
            f_copy(q, k).wait_recv()
        lhs = hid[q].reshape(side, chunk)

        @pl.when(c == 0)
        def _():
            acc[s] = jnp.zeros((side, width), jnp.float32)
            dl[s] = jnp.zeros((side, dl.shape[2]), jnp.float32)

        for first in range(0, width, step):
            acc[s, :, first : first + step] += jnp.dot(
                lhs, wdv[c, :, first : first + step], preferred_element_type=jnp.float32
            )
        dl[s] += dot_rows(lhs, div[c])

        @pl.when(c == nc - 1)
        def _():
            finish(s)

    def block_at(t):
        return pl.ds(pl.multiple_of(t * block, block), block)

    def o_copy(k):
        t = lax.rem(my_t + k, nt)
        return remote(
            osend.at[k - 1], orecv.at[k - 1], o_s.at[k - 1], o_r.at[k - 1],
            {"tensor": t, "dp": my_d},
        )

    def l_target(m):
        u = lax.rem((my_t + nt // 2) * owners + m, slots)
        return u, lax.div(u, owners) * nd + lax.rem(u, owners) * 2 + 1

    def l_copy(m):
        u, index = l_target(m)
        return remote(straight.at[u], land.at[me], l_s.at[m], l_r.at[me], place(index))

    def l_start(m):
        u, index = l_target(m)

        @pl.when(index != me)
        def _():
            l_copy(m).start()

        @pl.when(index == me)
        def _():
            land[me] = straight[u]

    def l_sent(m):
        u, index = l_target(m)

        @pl.when(index != me)
        def _():
            l_copy(m).wait_send()

    def finish(s):
        @pl.when(s == 0)
        def _():
            for copy in out_maps:
                copy.wait()

        low = dl[s]
        high = low.astype(jnp.bfloat16)
        rest = low - high.astype(jnp.float32)
        middle = rest.astype(jnp.bfloat16)
        last = (rest - middle.astype(jnp.float32)).astype(jnp.bfloat16)
        terms = jnp.concatenate([high, middle, last], axis=1)
        for first in range(0, width, step):
            acc[s, :, first : first + step] += adapter_scale_factor * jnp.dot(
                terms, dov[:, first : first + step], preferred_element_type=jnp.float32
            )

        @pl.when(s == 0)
        def _():
            def o_send(k):
                osend[k - 1] = acc[0, block_at(lax.rem(my_t + k, nt)), :].astype(jnp.bfloat16)
                o_copy(k).start()

            each(1, nt, o_send)

        @pl.when(s == 1)
        def _():
            straight[...] = acc[1].reshape(slots, tok_dev, width).astype(jnp.bfloat16)
            each(0, slots, l_start)

    mine = pl.ds(pl.multiple_of(my_d * width, 128), width)

    def z_copy(i):
        return remote(fin.at[i], out.at[:, mine], z_s.at[i], z_r.at[my_d], at_dp(2 * i))

    lags = (FIRST_LAGS, tuple(lag + GAP for lag in SECOND_LAGS))
    stages = [
        (stage, lags[s][at], s)
        for at, stage in enumerate((up_part, pair_sum, activate, forward, down_part))
        for s in range(HALVES)
    ]

    def turn(i, carry):
        for stage, lag, part_of in stages:
            q = i - lag
            low, high = part_of * nc, (part_of + 1) * nc
            pl.when(jnp.logical_and(q >= low, q < high))(functools.partial(stage, q))
        return carry

    lax.fori_loop(0, max(nc + lags[0][-1], items + lags[1][-1]), turn, 0)

    def o_take(k):
        o_copy(k).wait_recv()
        acc[0, block_at(my_t), :] += orecv[k - 1].astype(jnp.float32)

    each(1, nt, o_take)
    fin[...] = acc[0, block_at(my_t), :].reshape(owners, tok_dev, width).astype(jnp.bfloat16)
    for i in range(owners):
        @pl.when(my_d != 2 * i)
        def _():
            z_copy(i).start()

        @pl.when(my_d == 2 * i)
        def _():
            out[:, mine] = fin[i]

    each(0, n, tok_sent)
    for s in range(HALVES):
        for k in range(1, nd):
            low_copy(s, k).wait_send()

    def drain(q):
        a_copy(q).wait_send()
        p_copy(q).wait_send()
        for k in range(1, half):
            b_copy(q, k).wait_send()
            h_copy(q, k).wait_send()
            f_copy(q, k).wait_send()

    each(0, items, drain)
    @pl.when(my_b == 1)
    def _():
        def l_wait(index):
            @pl.when(index != me)
            def _():
                remote(
                    straight.at[0], land.at[index], l_s.at[0], l_r.at[index], place(index)
                ).wait_recv()

        each(0, n, l_wait)
        for d in range(nd):
            total = land[d].astype(jnp.float32)
            for t in range(1, nt):
                total = total + land[t * nd + d].astype(jnp.float32)
            out[:, d * width : (d + 1) * width] = total.astype(jnp.bfloat16)

    each(1, nt, lambda k: o_copy(k).wait_send())
    each(0, slots, l_sent)

    for i in range(owners):
        @pl.when(my_d != 2 * i)
        def _():
            z_copy(i).wait_send()

    @pl.when(my_b == 0)
    def _():
        def z_wait(d):
            @pl.when(d != my_d)
            def _():
                place_of = pl.ds(pl.multiple_of(d * width, 128), width)
                remote(fin.at[0], out.at[:, place_of], z_s.at[0], z_r.at[d], at_dp(d)).wait_recv()

        each(0, nd, z_wait)


def body(tok, wg, wu, wd, ag, go, au, uo, di, do):
    nt = lax.axis_size("tensor")
    nd = lax.axis_size("dp")
    n = nt * nd
    half = nd // 2
    tok_dev = tok.shape[0]
    depth, hidden = wg.shape
    width = wd.shape[1]
    rank = ag.shape[1]
    chunk = 512 if hidden % 512 == 0 else hidden
    nc = hidden // chunk
    total = n * tok_dev
    side = total // HALVES
    rows = side // nd
    owners = nd // HALVES
    block = owners * tok_dev
    items = HALVES * nc
    far = half - 1
    bf, f32 = jnp.bfloat16, jnp.float32
    vm, dma = pltpu.VMEM, pltpu.SemaphoreType.DMA
    scratch = [
        vm((tok_dev, depth * nd), bf), vm((n, tok_dev, depth), bf), vm((HALVES, side, depth), bf),
        vm((nc, depth, chunk), bf), vm((nc, depth, chunk), bf), vm((nc, chunk, width), bf),
        vm((rank, depth), bf), vm((rank, depth), bf),
        vm((nc, rank, chunk), bf), vm((nc, rank, chunk), bf), vm((nc, rank, chunk), bf),
        vm((3 * rank, width), bf),
        vm((HALVES, nd, 2, rows, rank), f32), vm((HALVES, nd - 1, 2, rows, rank), f32),
        vm((HALVES, 2, nc, rows, chunk), f32),
        vm((items, 2, side // 2, chunk), f32),
        vm((items, 2, side // 2, chunk), bf), vm((items, 2, side // 2, chunk), bf),
        vm((items, far, 2, rows, chunk), bf), vm((items, far, 2, rows, chunk), bf),
        vm((items, nd, rows, chunk), bf),
        vm((HALVES, side, width), f32), vm((HALVES, side, rank), f32),
        vm((nt - 1, block, width), bf), vm((nt - 1, block, width), bf),
        vm((owners, tok_dev, width), bf),
        vm((nt * owners, tok_dev, width), bf), vm((n, tok_dev, width), bf),
        dma((6, nc)), dma((7,)), dma((n,)), dma((n,)),
        dma((HALVES, nd - 1)), dma((HALVES, nd - 1)),
        dma((items,)), dma((items,)), dma((items, far)), dma((items, far)),
        dma((items, far)), dma((items, far)), dma((items,)), dma((items,)),
        dma((items, far)), dma((items, far)),
        dma((nt - 1,)), dma((nt - 1,)), dma((owners,)), dma((nd,)),
        dma((nt * owners,)), dma((n,)),
    ]
    return pl.pallas_call(
        functools.partial(kernel, nt, nd, nc),
        out_shape=jax.ShapeDtypeStruct((tok_dev, width * nd), bf),
        in_specs=[pl.BlockSpec(memory_space=pl.ANY)] * 10,
        out_specs=pl.BlockSpec(memory_space=pltpu.VMEM),
        scratch_shapes=scratch,
        compiler_params=pltpu.CompilerParams(
            collective_id=0, has_side_effects=True, vmem_limit_bytes=67043328
        ),
    )(tok, wg, wu, wd, ag.T, go, au.T, uo, di.T, do)


def solution(mesh):
    placed = (
        P(("groups", "tensor", "dp"), None),
        P("dp", "tensor"),
        P("dp", "tensor"),
        P("tensor", "dp"),
        P(("groups", "dp"), None),
        P(None, ("groups", "tensor")),
        P(("groups", "dp"), None),
        P(None, ("groups", "tensor")),
        P(("groups", "tensor"), None),
        P(None, "groups"),
    )
    return jax.shard_map(
        body,
        mesh=mesh,
        in_specs=placed,
        out_specs=P(("groups", "tensor", "dp"), None),
        check_vma=False,
    )
```

```python
import functools

import jax
import jax.numpy as jnp
from jax import lax
from jax.experimental import pallas as pl
from jax.experimental.pallas import tpu as pltpu
from jax.sharding import PartitionSpec as P

adapter_scale_factor = 0.5
MESH = pl.DeviceIdType.MESH
HALVES = 2
EARLY = 1
FIRST_LAGS = (0, 1, 5, 9, 12)
SECOND_LAGS = (0, 2, 5, 9, 12)
GAP = 0


def dot_rows(a, b):
    return lax.dot_general(a, b, (((1,), (1,)), ((), ())), preferred_element_type=jnp.float32)


def kernel(
    nt, nd, nc,
    tok, wg, wu, wd, ag, go, au, uo, di, do, out,
    tokv, xbuf, x, wgv, wuv, wdv, agv, auv, gov, uov, div, dov,
    lowp, lowr, added, part, send_a, recv_a, send_b, recv_b, hid, acc, dl,
    osend, orecv, fin, straight, land,
    wsem, ssem, tok_s, tok_r, low_s, low_r, a_s, a_r, b_s, b_r,
    h_s, h_r, p_s, p_r, f_s, f_r, o_s, o_r, z_s, z_r, l_s, l_r,
):
    n = nt * nd
    half = nd // 2
    depth = wg.shape[0]
    chunk = wgv.shape[2]
    width = wd.shape[1]
    rank = agv.shape[0]
    tok_dev = tok.shape[0]
    total_rows = n * tok_dev
    side = total_rows // HALVES
    rows = side // nd
    owners = nd // HALVES
    block = owners * tok_dev
    slots = nt * owners
    per_block = slots // nd
    items = HALVES * nc
    my_t = lax.axis_index("tensor")
    my_d = lax.axis_index("dp")
    me = my_t * nd + my_d
    my_j = lax.div(my_d, 2)
    my_b = lax.rem(my_d, 2)
    other_b = 1 - my_b
    mate = my_j * 2 + other_b

    def slot_of(index, parity):
        t, d = lax.div(index, nd), lax.rem(index, nd)
        u = t * owners + lax.div(d, 2)
        owner = lax.div(u, per_block)
        same = 1 - jnp.abs(lax.rem(owner, 2) - parity)
        at = same * half + lax.div(owner, 2)
        return lax.rem(d, 2) * slots + at * per_block + lax.rem(u, per_block)

    def each(low, high, act):
        def step(k, carry):
            act(k)
            return carry

        lax.fori_loop(low, high, step, 0)

    tok_in = pltpu.make_async_copy(tok, tokv, ssem.at[0])
    own_in = pltpu.make_async_copy(
        tok.at[:, pl.ds(pl.multiple_of(my_d * depth, 128), depth)],
        xbuf.at[slot_of(me, my_b)],
        ssem.at[1],
    )
    low_in = [
        pltpu.make_async_copy(ag, agv, ssem.at[2]),
        pltpu.make_async_copy(au, auv, ssem.at[3]),
    ]
    out_maps = [
        pltpu.make_async_copy(
            do.at[:, pl.ds(pl.multiple_of(my_d * width, 128), width)],
            dov.at[i * rank : (i + 1) * rank, :],
            ssem.at[4 + i],
        )
        for i in range(3)
    ]

    def cols(ref, c):
        return ref.at[:, c * chunk : (c + 1) * chunk]

    def rows_of(ref, c):
        return ref.at[c * chunk : (c + 1) * chunk, :]

    plan = (
        (wg, wgv, cols), (wu, wuv, cols), (go, gov, cols), (uo, uov, cols),
        (wd, wdv, rows_of), (di, div, cols),
    )

    def load(kind, static_c, c):
        src, dst, cut = plan[kind]
        return pltpu.make_async_copy(cut(src, static_c), dst.at[c], wsem.at[kind, c])

    tok_in.start()
    own_in.start()
    for copy in low_in:
        copy.start()
    early = min(EARLY, nc)

    def load_up(low, high):
        for c in range(low, high):
            for kind in range(4):
                load(kind, c, c).start()

    load_up(0, early)
    barrier = pltpu.get_barrier_semaphore()

    def place(index):
        return {"tensor": lax.div(index, nd), "dp": lax.rem(index, nd)}

    def greet(k):
        pl.semaphore_signal(
            barrier, inc=1, device_id=place(lax.rem(me + k, n)), device_id_type=MESH
        )

    each(1, n, greet)
    tok_in.wait()
    pl.semaphore_wait(barrier, n - 1)

    def remote(src, dst, send_sem, recv_sem, device):
        return pltpu.make_async_remote_copy(
            src_ref=src, dst_ref=dst, send_sem=send_sem, recv_sem=recv_sem,
            device_id=device, device_id_type=MESH,
        )

    def at_dp(d):
        return {"tensor": my_t, "dp": d}

    first_off = (nt // 2) * nd

    def tok_target(k):
        return lax.rem(me + first_off + k, n)

    def tok_copy(k):
        index = tok_target(k)
        d = lax.rem(index, nd)
        return remote(
            tokv.at[:, pl.ds(pl.multiple_of(d * depth, 128), depth)],
            xbuf.at[slot_of(me, lax.rem(d, 2))],
            tok_s.at[k], tok_r.at[me], place(index),
        )

    def tok_start(k):
        @pl.when(tok_target(k) != me)
        def _():
            tok_copy(k).start()

    def tok_sent(k):
        @pl.when(tok_target(k) != me)
        def _():
            tok_copy(k).wait_send()

    def tok_wait(s):
        def one(u):
            index = lax.div(u, owners) * nd + lax.rem(u, owners) * 2 + s

            @pl.when(index != me)
            def _():
                remote(
                    tokv.at[:, pl.ds(0, depth)], xbuf.at[slot_of(index, my_b)],
                    tok_s.at[0], tok_r.at[index], place(index),
                ).wait_recv()

        each(0, slots, one)

    def gather_rows(s):
        x[s] = (
            xbuf[pl.ds(s * slots, slots)].astype(jnp.float32).reshape(side, depth).astype(jnp.bfloat16)
        )

    @pl.when(my_b == 0)
    def _():
        each(0, n, tok_start)

    load_up(early, nc)

    own_in.wait()
    tok_wait(0)

    @pl.when(my_b == 1)
    def _():
        each(0, n, tok_start)

    def low_at(d):
        return (1 - jnp.abs(lax.rem(d, 2) - my_b)) * half + lax.div(d, 2)

    def low_copy(s, k):
        d = lax.rem(my_d + k, nd)
        return remote(
            lowp.at[s, low_at(d)], lowr.at[s, k - 1], low_s.at[s, k - 1], low_r.at[s, k - 1],
            at_dp(d),
        )

    def low_part(s):
        @pl.when(s == 0)
        def _():
            for copy in low_in:
                copy.wait()

        for which, ref in ((0, agv), (1, auv)):
            low = dot_rows(x[s], ref[...])
            for d in range(nd):
                lowp[s, d, which] = low[d * rows : (d + 1) * rows]
        for k in range(1, nd):
            low_copy(s, k).start()

    def a_copy(q):
        return remote(send_a.at[q], recv_a.at[q], a_s.at[q], a_r.at[q], at_dp(mate))

    def ahead(k):
        return lax.rem(my_j + k, half)

    def behind(k):
        return lax.rem(my_j + half - k, half) * 2 + my_b

    def b_copy(q, k):
        return remote(
            send_b.at[q, k - 1], recv_b.at[q, k - 1],
            b_s.at[q, k - 1], b_r.at[q, k - 1], at_dp(ahead(k) * 2 + my_b),
        )

    def h_copy(q, k):
        return remote(
            hid.at[q, my_d], hid.at[q, my_d],
            h_s.at[q, k - 1], h_r.at[q, k - 1], at_dp(ahead(k) * 2 + my_b),
        )

    def p_copy(q):
        return remote(hid.at[q, my_d], hid.at[q, my_d], p_s.at[q], p_r.at[q], at_dp(mate))

    def f_copy(q, k):
        return remote(
            hid.at[q, behind(k)], hid.at[q, behind(k)],
            f_s.at[q, k - 1], f_r.at[q, k - 1], at_dp(mate),
        )

    def rows_at(j):
        return pl.ds(pl.multiple_of(j * rows, rows), rows)

    def split(q):
        return lax.div(q, nc), lax.rem(q, nc)

    piece = 128 if chunk % 128 == 0 else chunk

    def up_part(q):
        s, c = split(q)

        @pl.when(q == nc)
        def _():
            tok_wait(1)

        @pl.when(c == 0)
        def _():
            gather_rows(s)

        @pl.when(s == 0)
        def _():
            load(0, 0, c).wait()
            load(1, 0, c).wait()

        for which, ref in ((0, wgv), (1, wuv)):
            for first in range(0, chunk, piece):
                at = slice(first, first + piece)
                value = jnp.dot(x[s], ref[c, :, at], preferred_element_type=jnp.float32)
                send_a[q, which, :, at] = value[: side // 2].astype(jnp.bfloat16)
                part[q, which, :, at] = value[side // 2 :]
        a_copy(q).start()

        @pl.when(q == 0)
        def _():
            for at in range(nc):
                for kind in range(4, 6):
                    load(kind, at, at).start()
            for copy in out_maps:
                copy.start()

        @pl.when(c == 0)
        def _():
            low_part(s)

    def pair_sum(q):
        a_copy(q).wait_recv()
        for k in range(1, half):
            at = rows_at(ahead(k))
            for which in range(2):
                send_b[q, k - 1, which] = (
                    part[q, which, at, :] + recv_a[q, which, at, :].astype(jnp.float32)
                ).astype(jnp.bfloat16)
            b_copy(q, k).start()

    def activate(q):
        s, c = split(q)

        @pl.when(c == 0)
        def _():
            for k in range(1, nd):
                low_copy(s, k).wait_recv()

            @pl.when(s == 0)
            def _():
                for at in range(nc):
                    load(2, at, at).wait()
                    load(3, at, at).wait()

            total = lowp[s, half + my_j]
            for k in range(1, nd):
                total = total + lowr[s, k - 1]
            low = total.astype(jnp.bfloat16)
            for which, ref in ((0, gov), (1, uov)):
                for at in range(nc):
                    added[s, which, at] = adapter_scale_factor * jnp.dot(
                        low[which], ref[at], preferred_element_type=jnp.float32
                    )

        for k in range(1, half):
            b_copy(q, k).wait_recv()
        sums = []
        at = rows_at(my_j)
        for which in range(2):
            value = added[s, which, c] + part[q, which, at, :] + recv_a[q, which, at, :].astype(jnp.float32)
            for k in range(1, half):
                value = value + recv_b[q, k - 1, which].astype(jnp.float32)
            sums.append(value)
        gate, up = sums
        hid[q, my_d] = (gate / (1.0 + jnp.exp(-gate)) * up).astype(jnp.bfloat16)
        for k in range(1, half):
            h_copy(q, k).start()
        p_copy(q).start()

    def forward(q):
        for k in range(1, half):
            h_copy(q, k).wait_recv()
            f_copy(q, k).start()

    step = 512 if width % 512 == 0 else width

    def down_part(q):
        s, c = split(q)

        @pl.when(s == 0)
        def _():
            load(4, 0, c).wait()
            load(5, 0, c).wait()

        p_copy(q).wait_recv()
        for k in range(1, half):
            f_copy(q, k).wait_recv()
        lhs = hid[q].reshape(side, chunk)

        @pl.when(c == 0)
        def _():
            acc[s] = jnp.zeros((side, width), jnp.float32)
            dl[s] = jnp.zeros((side, dl.shape[2]), jnp.float32)

        for first in range(0, width, step):
            acc[s, :, first : first + step] += jnp.dot(
                lhs, wdv[c, :, first : first + step], preferred_element_type=jnp.float32
            )
        dl[s] += dot_rows(lhs, div[c])

        @pl.when(c == nc - 1)
        def _():
            finish(s)

    def block_at(t):
        return pl.ds(pl.multiple_of(t * block, block), block)

    def o_copy(k):
        t = lax.rem(my_t + k, nt)
        return remote(
            osend.at[k - 1], orecv.at[k - 1], o_s.at[k - 1], o_r.at[k - 1],
            {"tensor": t, "dp": my_d},
        )

    def l_target(m):
        u = lax.rem((my_t + nt // 2) * owners + m, slots)
        return u, lax.div(u, owners) * nd + lax.rem(u, owners) * 2 + 1

    def l_copy(m):
        u, index = l_target(m)
        return remote(straight.at[u], land.at[me], l_s.at[m], l_r.at[me], place(index))

    def l_start(m):
        u, index = l_target(m)

        @pl.when(index != me)
        def _():
            l_copy(m).start()

        @pl.when(index == me)
        def _():
            land[me] = straight[u]

    def l_sent(m):
        u, index = l_target(m)

        @pl.when(index != me)
        def _():
            l_copy(m).wait_send()

    def finish(s):
        @pl.when(s == 0)
        def _():
            for copy in out_maps:
                copy.wait()

        low = dl[s]
        high = low.astype(jnp.bfloat16)
        rest = low - high.astype(jnp.float32)
        middle = rest.astype(jnp.bfloat16)
        last = (rest - middle.astype(jnp.float32)).astype(jnp.bfloat16)
        terms = jnp.concatenate([high, middle, last], axis=1)
        for first in range(0, width, step):
            acc[s, :, first : first + step] += adapter_scale_factor * jnp.dot(
                terms, dov[:, first : first + step], preferred_element_type=jnp.float32
            )

        @pl.when(s == 0)
        def _():
            def o_send(k):
                osend[k - 1] = acc[0, block_at(lax.rem(my_t + k, nt)), :].astype(jnp.bfloat16)
                o_copy(k).start()

            each(1, nt, o_send)

        @pl.when(s == 1)
        def _():
            straight[...] = acc[1].reshape(slots, tok_dev, width).astype(jnp.bfloat16)
            each(0, slots, l_start)

    mine = pl.ds(pl.multiple_of(my_d * width, 128), width)

    def z_copy(i):
        return remote(fin.at[i], out.at[:, mine], z_s.at[i], z_r.at[my_d], at_dp(2 * i))

    lags = (FIRST_LAGS, tuple(lag + GAP for lag in SECOND_LAGS))
    stages = [
        (stage, lags[s][at], s)
        for at, stage in enumerate((up_part, pair_sum, activate, forward, down_part))
        for s in range(HALVES)
    ]

    def turn(i, carry):
        for stage, lag, part_of in stages:
            q = i - lag
            low, high = part_of * nc, (part_of + 1) * nc
            pl.when(jnp.logical_and(q >= low, q < high))(functools.partial(stage, q))
        return carry

    lax.fori_loop(0, max(nc + lags[0][-1], items + lags[1][-1]), turn, 0)

    def o_take(k):
        o_copy(k).wait_recv()
        acc[0, block_at(my_t), :] += orecv[k - 1].astype(jnp.float32)

    each(1, nt, o_take)
    fin[...] = acc[0, block_at(my_t), :].reshape(owners, tok_dev, width).astype(jnp.bfloat16)
    for i in range(owners):
        @pl.when(my_d != 2 * i)
        def _():
            z_copy(i).start()

        @pl.when(my_d == 2 * i)
        def _():
            out[:, mine] = fin[i]

    each(0, n, tok_sent)
    for s in range(HALVES):
        for k in range(1, nd):
            low_copy(s, k).wait_send()

    def drain(q):
        a_copy(q).wait_send()
        p_copy(q).wait_send()
        for k in range(1, half):
            b_copy(q, k).wait_send()
            h_copy(q, k).wait_send()
            f_copy(q, k).wait_send()

    each(0, items, drain)
    @pl.when(my_b == 1)
    def _():
        def l_wait(index):
            @pl.when(index != me)
            def _():
                remote(
                    straight.at[0], land.at[index], l_s.at[0], l_r.at[index], place(index)
                ).wait_recv()

        each(0, n, l_wait)
        for d in range(nd):
            total = land[d].astype(jnp.float32)
            for t in range(1, nt):
                total = total + land[t * nd + d].astype(jnp.float32)
            out[:, d * width : (d + 1) * width] = total.astype(jnp.bfloat16)

    each(1, nt, lambda k: o_copy(k).wait_send())
    each(0, slots, l_sent)

    for i in range(owners):
        @pl.when(my_d != 2 * i)
        def _():
            z_copy(i).wait_send()

    @pl.when(my_b == 0)
    def _():
        def z_wait(d):
            @pl.when(d != my_d)
            def _():
                place_of = pl.ds(pl.multiple_of(d * width, 128), width)
                remote(fin.at[0], out.at[:, place_of], z_s.at[0], z_r.at[d], at_dp(d)).wait_recv()

        each(0, nd, z_wait)


def body(tok, wg, wu, wd, ag, go, au, uo, di, do):
    nt = lax.axis_size("tensor")
    nd = lax.axis_size("dp")
    n = nt * nd
    half = nd // 2
    tok_dev = tok.shape[0]
    depth, hidden = wg.shape
    width = wd.shape[1]
    rank = ag.shape[1]
    chunk = 512 if hidden % 512 == 0 else hidden
    nc = hidden // chunk
    total = n * tok_dev
    side = total // HALVES
    rows = side // nd
    owners = nd // HALVES
    block = owners * tok_dev
    items = HALVES * nc
    far = half - 1
    bf, f32 = jnp.bfloat16, jnp.float32
    vm, dma = pltpu.VMEM, pltpu.SemaphoreType.DMA
    scratch = [
        vm((tok_dev, depth * nd), bf), vm((n, tok_dev, depth), bf), vm((HALVES, side, depth), bf),
        vm((nc, depth, chunk), bf), vm((nc, depth, chunk), bf), vm((nc, chunk, width), bf),
        vm((rank, depth), bf), vm((rank, depth), bf),
        vm((nc, rank, chunk), bf), vm((nc, rank, chunk), bf), vm((nc, rank, chunk), bf),
        vm((3 * rank, width), bf),
        vm((HALVES, nd, 2, rows, rank), f32), vm((HALVES, nd - 1, 2, rows, rank), f32),
        vm((HALVES, 2, nc, rows, chunk), f32),
        vm((items, 2, side // 2, chunk), f32),
        vm((items, 2, side // 2, chunk), bf), vm((items, 2, side // 2, chunk), bf),
        vm((items, far, 2, rows, chunk), bf), vm((items, far, 2, rows, chunk), bf),
        vm((items, nd, rows, chunk), bf),
        vm((HALVES, side, width), f32), vm((HALVES, side, rank), f32),
        vm((nt - 1, block, width), bf), vm((nt - 1, block, width), bf),
        vm((owners, tok_dev, width), bf),
        vm((nt * owners, tok_dev, width), bf), vm((n, tok_dev, width), bf),
        dma((6, nc)), dma((7,)), dma((n,)), dma((n,)),
        dma((HALVES, nd - 1)), dma((HALVES, nd - 1)),
        dma((items,)), dma((items,)), dma((items, far)), dma((items, far)),
        dma((items, far)), dma((items, far)), dma((items,)), dma((items,)),
        dma((items, far)), dma((items, far)),
        dma((nt - 1,)), dma((nt - 1,)), dma((owners,)), dma((nd,)),
        dma((nt * owners,)), dma((n,)),
    ]
    return pl.pallas_call(
        functools.partial(kernel, nt, nd, nc),
        out_shape=jax.ShapeDtypeStruct((tok_dev, width * nd), bf),
        in_specs=[pl.BlockSpec(memory_space=pl.ANY)] * 10,
        out_specs=pl.BlockSpec(memory_space=pltpu.VMEM),
        scratch_shapes=scratch,
        compiler_params=pltpu.CompilerParams(
            collective_id=0, has_side_effects=True, vmem_limit_bytes=67043328
        ),
    )(tok, wg, wu, wd, ag.T, go, au.T, uo, di.T, do)


def solution(mesh):
    placed = (
        P(("groups", "tensor", "dp"), None),
        P("dp", "tensor"),
        P("dp", "tensor"),
        P("tensor", "dp"),
        P(("groups", "dp"), None),
        P(None, ("groups", "tensor")),
        P(("groups", "dp"), None),
        P(None, ("groups", "tensor")),
        P(("groups", "tensor"), None),
        P(None, "groups"),
    )
    return jax.shard_map(
        body,
        mesh=mesh,
        in_specs=placed,
        out_specs=P(("groups", "tensor", "dp"), None),
        check_vma=False,
    )
```
